32 devices in a mesh: groups: 2 (over x), span: 16 (over z, y, core).
Axes of the slice: x: 2, y: 2, z: 4, core: 2. Of those that a mesh axis runs over, the one named last changes fastest.
Arguments:
- hidden_in: bfloat16 [16384, 2240], P(('groups', 'span')), parts along dimension 0, may hold values from -16 to 16
- noisy_latents: float32 [16384, 32], P(('groups', 'span')), parts along dimension 0, may hold values from -6 to 6
- span_ids: int32 [16384], P(('groups', 'span')), parts along dimension 0, may hold values from 0 to 31, as said below
- tile_map: int32 [16384], P('groups'), parts along dimension 0, may hold values from 0 to 8191, as said below
- qkv_weight: bfloat16 [2240, 3360], replicated, may hold values from -0.125 to 0.125
- out_weight: bfloat16 [1120, 2240], replicated, may hold values from -0.1875 to 0.1875
- norm_gain: float32 [2240], replicated, may hold values from 0.1 to 1.9
- velocity_weight: bfloat16 [2240, 32], replicated, may hold values from -0.125 to 0.125
- conv_first: bfloat16 [3, 3, 32, 256], replicated, may hold values from -0.375 to 0.375
- conv_second: bfloat16 [3, 3, 256, 256], replicated, may hold values from -0.125 to 0.125
Outputs:
- new_latents: float32 [16384, 32], P(('groups', 'span')), parts along dimension 0
- decoded: bfloat16 [256, 64, 256], P(('groups', 'span')), parts along dimension 0
The draws below stay inside these ranges and needn't reach their ends.
There are 2 independent parts, one for each index of `groups`. The reference program is written for one: setup_inputs(seed, part) draws one part's arguments, and reference() takes and returns one part's arrays. A program takes and returns all parts, laid end to end along the dimension named above; an argument that names none is the same for every part. Nothing has to cross between parts.
Inputs may be any that keep to these rules, and one draw needn't show every extreme that they name: `span_ids`: never falling along the tokens; every span number occurs, each span holds 1 to 1024 tokens, and one span holds exactly 1024. `tile_map`: A permutation of the 8192 grid positions; the 512 tokens of each aligned block of tokens place exactly 32 tokens in each aligned block of 512 positions.
All inputs are finite; a program needn't handle non-finite values.
Results may differ from the reference program's by a relative error of at most 0.01.
Values may be sent and summed in bfloat16 or wider, within the bound.
A program may use at most 128 MiB of HBM per device.

```python
import math
import jax
import jax.numpy as jnp
from jax import lax

D = 2240
HEADS = 35
HDIM = 32
C = 32
CH = 256
IW = 64
TOK_DEV = 512
TOKENS = 8192
ROWS = 128
NSEG = 32
HD = 1120
N_SPAN = 16


def draw_hidden_in(key, part):
    key = jax.random.fold_in(key, 101)
    keys = jax.random.split(key, 4)
    scene_count = TOKENS // IW
    scene = jax.random.normal(keys[1], (scene_count, D), jnp.float32)
    scene_rows = jnp.repeat(scene, IW, axis=0)
    columns = jnp.exp(jax.random.uniform(keys[2], (D,), jnp.float32, math.log(0.3), math.log(3.0)))
    noise = jax.random.normal(keys[0], (TOKENS, D), jnp.float32)
    row_scale = jnp.exp(jax.random.uniform(keys[3], (TOKENS, 1), jnp.float32, math.log(0.1), math.log(1.0)))
    base = (0.7 * noise + 2.5 * scene_rows) * row_scale
    return jnp.clip(base * columns, -16.0, 16.0).astype(jnp.bfloat16)


def draw_span_ids(key, part):
    key = jax.random.fold_in(key, 303)
    long_key, extra_key, offset_key, align_key = jax.random.split(key, 4)
    devices = N_SPAN
    per_device = TOK_DEV
    long_dev = jax.random.randint(long_key, (), 1, min(4, devices - 2), jnp.int32)
    extra_dev = jax.random.randint(extra_key, (), 0, devices, jnp.int32)
    extra_dev = jnp.where((extra_dev == long_dev) | (extra_dev == long_dev + 1), (extra_dev + 2) % devices, extra_dev)
    offsets = jax.vmap(lambda single: jax.random.permutation(single, per_device - 1)[:3])(jax.random.split(offset_key, devices)).astype(jnp.int32) + 1
    device_no = jnp.arange(devices, dtype=jnp.int32)
    aligned = jax.random.randint(align_key, (devices,), 0, 2, jnp.int32)
    may_align = (device_no >= 1) & (device_no != long_dev + 2) & (aligned == 1)
    offsets = offsets.at[:, 0].set(jnp.where(may_align, 0, offsets[:, 0]))
    taken = jnp.where((device_no == long_dev) | (device_no == long_dev + 1), 0, jnp.where(device_no == extra_dev, 3, 2))
    used = jnp.arange(3, dtype=jnp.int32)[None, :] < taken[:, None]
    spots = jnp.where(used, device_no[:, None] * per_device + offsets, devices * per_device).astype(jnp.int32)
    starts = jnp.zeros((devices * per_device + 1,), jnp.int32).at[spots.reshape(-1)].set(1)
    bounds = jnp.stack([long_dev * per_device, (long_dev + 2) * per_device]).astype(jnp.int32)
    starts = starts.at[bounds].set(1)
    return jnp.cumsum(starts[:devices * per_device]).astype(jnp.int32)


def draw_tile_map(key, part):
    key = jax.random.fold_in(key, 202)
    send_key, recv_key = jax.random.split(key)
    count = N_SPAN
    block = TOK_DEV
    share = block // count
    sender = jax.vmap(lambda one: jax.random.permutation(one, block))(jax.random.split(send_key, count))
    receiver = jax.vmap(lambda one: jax.random.permutation(one, block))(jax.random.split(recv_key, count))
    source = jnp.arange(count, dtype=jnp.int32)[:, None, None]
    target = jnp.arange(count, dtype=jnp.int32)[None, :, None]
    within = jnp.arange(share, dtype=jnp.int32)[None, None, :]
    token = source * block + sender[source, target * share + within]
    place = target * block + receiver[target, source * share + within]
    result = jnp.zeros((count * block,), jnp.int32).at[token.reshape(-1)].set(place.reshape(-1).astype(jnp.int32))
    return result


def block_levels(own_key, shape, shards, low, largest):
    def one(axis_at, shards_of):
        steps = jax.random.uniform(jax.random.fold_in(jax.random.fold_in(own_key, 6), axis_at), (shards_of,), jnp.float32, low / len(shards), largest / len(shards))
        return jnp.repeat(jnp.exp(steps), shape[axis_at] // shards_of).reshape((-1,) + (1,) * (len(shape) - axis_at - 1))

    level = one(*shards[0])
    for cut in shards[1:]:
        level = level * one(*cut)
    return level


def centred(stream_key, shape, deviation, limit, pieces=(), kind=jnp.bfloat16):
    drawn = deviation * jax.random.normal(stream_key, shape, jnp.float32)
    if pieces:
        drawn = drawn * block_levels(stream_key, shape, pieces, -0.22, 0.18)
    return jnp.clip(drawn, -limit, limit).astype(kind)


def setup_inputs(seed: int = 0, part: int = 0) -> dict:
    streams_of = jax.random.split(jax.random.key(seed), 11)
    part_keys = jax.random.split(jax.random.fold_in(streams_of[10], part), 11)
    hidden_in = draw_hidden_in(jax.random.fold_in(jax.random.fold_in(streams_of[10], part), 71), part)
    noisy_latents = centred(part_keys[1], (TOKENS, C), 1.0, 6.0, ((0, 16),), jnp.float32)
    span_ids = draw_span_ids(jax.random.fold_in(jax.random.fold_in(streams_of[10], part), 71), part)
    tile_map = draw_tile_map(jax.random.fold_in(jax.random.fold_in(streams_of[10], part), 71), part)
    qkv_weight = centred(streams_of[4], (D, 3 * HD), D ** -0.5, 0.125)
    out_weight = centred(streams_of[5], (HD, D), HD ** -0.5, 0.1875)
    norm_gain = jnp.clip(1.0 + 0.18 * jax.random.normal(streams_of[6], (D,), jnp.float32), 0.1, 1.9)
    velocity_weight = centred(streams_of[7], (D, C), D ** -0.5, 0.125)
    conv_first = centred(streams_of[8], (3, 3, C, CH), (9 * C) ** -0.5, 0.375)
    conv_second = centred(streams_of[9], (3, 3, CH, CH), (9 * CH) ** -0.5, 0.125)
    return dict(hidden_in=hidden_in, noisy_latents=noisy_latents, span_ids=span_ids, tile_map=tile_map, qkv_weight=qkv_weight, out_weight=out_weight, norm_gain=norm_gain, velocity_weight=velocity_weight, conv_first=conv_first, conv_second=conv_second)


def conv_rows(padded, weight):
    height = padded.shape[0] - 2
    width = padded.shape[1]
    framed = jnp.pad(padded, ((0, 0), (1, 1), (0, 0)))
    patches = jnp.concatenate([framed[row_off:row_off + height, col_off:col_off + width, :] for row_off in range(3) for col_off in range(3)], axis=2)
    inputs = weight.shape[2]
    result = jnp.dot(patches.reshape(height * width, 9 * inputs), weight.reshape(9 * inputs, weight.shape[3]), preferred_element_type=jnp.float32)
    return result.reshape(height, width, weight.shape[3])

def reference(hidden_in, noisy_latents, span_ids, tile_map, qkv_weight, out_weight, norm_gain, velocity_weight, conv_first, conv_second):
    inner = HEADS * HDIM
    packed = jnp.dot(hidden_in, qkv_weight, preferred_element_type=jnp.float32).astype(jnp.bfloat16)
    query = jnp.maximum(packed[:, :inner], 0).reshape(TOKENS, HEADS, HDIM)
    keys = jnp.maximum(packed[:, inner:2 * inner], 0).reshape(TOKENS, HEADS, HDIM)
    values = packed[:, 2 * inner:].reshape(TOKENS, HEADS, HDIM)
    visible = (span_ids[None, :] <= jnp.arange(NSEG, dtype=jnp.int32)[:, None]).astype(jnp.float32)

    def one_head(operands):
        query_h, keys_h, values_h = operands
        query_f = query_h.astype(jnp.float32)
        keys_f = keys_h.astype(jnp.float32)
        values_f = values_h.astype(jnp.float32)
        outer = (keys_f[:, :, None] * values_f[:, None, :]).reshape(TOKENS, HDIM * HDIM)
        states = jnp.dot(visible, outer, precision=lax.Precision.HIGHEST).reshape(NSEG, HDIM, HDIM)
        sums = jnp.dot(visible, keys_f, precision=lax.Precision.HIGHEST)
        numer = jnp.einsum('td,tde->te', query_f, states[span_ids], precision=lax.Precision.HIGHEST)
        denom = 1.0 + lax.optimization_barrier(jnp.sum(query_f * sums[span_ids], axis=1))
        return numer / denom[:, None]
    heads_out = lax.map(one_head, (jnp.transpose(query, (1, 0, 2)), jnp.transpose(keys, (1, 0, 2)), jnp.transpose(values, (1, 0, 2))))
    attention = jnp.transpose(heads_out, (1, 0, 2)).reshape(TOKENS, inner).astype(jnp.bfloat16)
    mixed = hidden_in.astype(jnp.float32) + jnp.dot(attention, out_weight, preferred_element_type=jnp.float32)
    meansq = lax.optimization_barrier(jnp.mean(mixed * mixed, axis=1, keepdims=True))
    normed = (mixed * lax.rsqrt(meansq + 1e-06) * norm_gain).astype(jnp.bfloat16)
    velocity = jnp.dot(normed, velocity_weight, preferred_element_type=jnp.float32)
    new_latents = noisy_latents - 0.5 * velocity
    tile = jnp.zeros((TOKENS, C), jnp.bfloat16).at[tile_map].set(new_latents.astype(jnp.bfloat16)).reshape(ROWS, IW, C)
    padded = jnp.pad(tile, ((1, 1), (0, 0), (0, 0)))
    first = jax.nn.silu(conv_rows(padded, conv_first)).astype(jnp.bfloat16)
    decoded = conv_rows(jnp.pad(first, ((1, 1), (0, 0), (0, 0))), conv_second).astype(jnp.bfloat16)
    return (new_latents, decoded)
```

```python
import functools

import jax
import jax.numpy as jnp
from jax import lax
from jax.experimental import pallas as pl
from jax.experimental.pallas import tpu as pltpu
from jax.sharding import PartitionSpec as P

HDIM = 32
IW = 64
BLK = 256
BF = jnp.bfloat16
F32 = jnp.float32


def dot(a, b):
    return jnp.dot(a, b, preferred_element_type=F32)


def dot_nt(a, b):
    return lax.dot_general(a, b, (((1,), (1,)), ((), ())), preferred_element_type=F32)


def dot_tn(a, b):
    return lax.dot_general(a, b, (((0,), (0,)), ((), ())), preferred_element_type=F32)


def iota(shape, axis):
    return lax.broadcasted_iota(jnp.int32, shape, axis)


def kernel(
    cfg,
    hid_hbm, noisy, span_ref, map_ref, wq_hbm, wo_hbm, gain, vw, w1, w2_hbm,
    lat_out, dec_out,
    hid, wq, wo, w2, packed, qs, ks, vs, num, kvis, att,
    st_c0, st_b0, st_send, lead_send, pair_recv, lead_recv, half_send, half_recv,
    fin_send, fin_recv, carry, after, onehot, posout, xlat, outgoing, incoming,
    wide, halo_send, halo_recv, first, shifted,
    wsem, lsem, psem, hsend, hrecv, fsem, lead_ssem, lead_rsem, asend, arecv, halo_ssem, halo_rsem,
):
    n, toks, d, inner, pad = cfg
    half = pad // 2
    chips = n // 2
    groups = pad // BLK
    me = lax.axis_index("span")
    core = lax.rem(me, 2)
    chip = me // 2
    partner = me + 1 - 2 * core
    share = toks // n
    chunk = toks // 2

    def remote(src, dst, ss, rs, dev):
        return pltpu.make_async_remote_copy(
            src_ref=src, dst_ref=dst, send_sem=ss, recv_sem=rs,
            device_id={"span": dev}, device_id_type=pl.DeviceIdType.MESH,
        )

    barrier = pltpu.get_barrier_semaphore()
    for k in range(1, n):
        pl.semaphore_signal(
            barrier, inc=1, device_id={"span": lax.rem(me + k, n)},
            device_id_type=pl.DeviceIdType.MESH,
        )

    total = wq_hbm.shape[1]
    full = total // BLK
    rest = total - full * BLK
    lo = inner // BLK

    def wcopy(b):
        cols = pl.ds(pl.multiple_of(b * BLK, BLK), BLK)
        return pltpu.make_async_copy(wq_hbm.at[:, cols], wq.at[:, cols], wsem.at[b])

    hcopy = pltpu.make_async_copy(hid_hbm, hid, lsem.at[0])
    hcopy.start()
    for b in range(lo, full):
        wcopy(b).start()
    tail_copy = None
    if rest:
        tail_copy = pltpu.make_async_copy(
            wq_hbm.at[:, full * BLK : total], wq.at[:, full * BLK : total], wsem.at[full]
        )
        tail_copy.start()
    for b in range(lo):
        wcopy(b).start()
    ocopy = pltpu.make_async_copy(wo_hbm, wo, lsem.at[1])
    ocopy.start()
    w2copy = pltpu.make_async_copy(w2_hbm, w2, lsem.at[2])
    w2copy.start()

    span_row = span_ref[...].astype(F32)
    span_col = jnp.transpose(jnp.broadcast_to(span_row, (128, toks)))[:, 0:1]
    first_seg = span_col[0:1, :]
    last_seg = span_col[toks - 1 : toks, :]
    lasts = [span_col[(c + 1) * chunk - 1 : (c + 1) * chunk, :] for c in range(2)]

    hcopy.wait()

    def project(b, carry_in):
        wcopy(b).wait()
        cols = pl.ds(pl.multiple_of(b * BLK, BLK), BLK)
        packed[:, cols] = dot(hid[...], wq[:, cols]).astype(BF)
        return carry_in

    lax.fori_loop(lo, full, project, 0)
    if rest:
        tail_copy.wait()
        packed[:, full * BLK : total] = dot(hid[...], wq[:, full * BLK : total]).astype(BF)

    def shift_in(dst, begin, relu):
        base = begin // 128 * 128
        off = begin - base
        width = packed.shape[1]
        end = min(base + pad + 128, width)

        def rows(r, c):
            rs = pl.ds(pl.multiple_of(r * 128, 128), 128)
            val = packed[rs, base:end].astype(F32)
            if off:
                val = pltpu.roll(val, val.shape[1] - off, 1)
            val = val[:, :pad]
            if relu:
                val = jnp.maximum(val, 0.0)
            val = jnp.where(iota((128, pad), 1) < inner, val, 0.0)
            dst[rs, :] = val.astype(BF)
            return c

        lax.fori_loop(0, toks // 128, rows, 0)

    shift_in(ks, inner, True)
    shift_in(vs, 2 * inner, False)

    block = (iota((BLK, BLK), 0) // HDIM == iota((BLK, BLK), 1) // HDIM)
    block_f = block.astype(F32)

    def compact(full_state):
        kept = jnp.where(block, full_state, 0.0)
        out = kept[0:HDIM]
        for h in range(1, BLK // HDIM):
            out = out + kept[h * HDIM : (h + 1) * HDIM]
        return out

    def expand(small):
        return (jnp.concatenate([small] * (BLK // HDIM), axis=0) * block_f).astype(BF)

    lead_col = (span_col == first_seg).astype(F32)
    to_b0 = (span_col[chunk:, :] <= lasts[0]).astype(F32)

    def states(g, c):
        cols = pl.ds(pl.multiple_of(g * BLK, BLK), BLK)
        k8 = ks[:, cols]
        v8 = vs[:, cols]
        s0 = compact(dot_tn(k8[:chunk], v8[:chunk]))
        s1 = compact(dot_tn(k8[chunk:], v8[chunk:]))
        k1 = (k8[chunk:].astype(F32) * to_b0).astype(BF)
        sb = compact(dot_tn(k1, v8[chunk:]))
        kl = (k8.astype(F32) * lead_col).astype(BF)
        sl = compact(dot_tn(kl, v8))
        st_c0[:, cols] = s0
        st_b0[:, cols] = s0 + sb
        num[0:HDIM, cols] = s0 + s1
        num[HDIM : 2 * HDIM, cols] = sl
        return c

    lax.fori_loop(0, groups, states, 0)

    def pack_sums(dst, column):
        kf = ks[...].astype(F32)
        if column is not None:
            kf = kf * column
        sums = jnp.sum(kf, axis=0, keepdims=True)
        parts = [sums[:, 128 * r : 128 * (r + 1)] for r in range((inner + 127) // 128)]
        base_rows = jnp.zeros((HDIM, 128), F32)
        row_no = iota((HDIM, 128), 0)
        for r, part in enumerate(parts):
            base_rows = jnp.where(row_no == r, jnp.broadcast_to(part, (HDIM, 128)), base_rows)
        base_rows = jnp.where(
            row_no == HDIM - 1, jnp.broadcast_to(first_seg, (HDIM, 128)), base_rows
        )
        dst[:, pad - 128 :] = base_rows.astype(BF)

    st_send[:, : pad - 128] = num[0:HDIM, : pad - 128].astype(BF)
    lead_send[:, : pad - 128] = num[HDIM : 2 * HDIM, : pad - 128].astype(BF)
    pack_sums(st_send, None)
    pack_sums(lead_send, lead_col)

    pl.semaphore_wait(barrier, n - 1)
    pair = remote(st_send, pair_recv, psem.at[0], psem.at[1], partner)
    pair.start()

    def lead_copy(k):
        return remote(
            lead_send, lead_recv.at[k], lead_ssem.at[k], lead_rsem.at[k],
            lax.rem(me - 1 - k + n, n),
        )

    for k in range(2):

        @pl.when(me >= k + 1)
        def _(k=k):
            lead_copy(k).start()

    mine = map_ref[pl.ds(me, 1), :]
    target = mine // toks
    within = mine - target * toks
    hits = (iota((n, toks), 0) == jnp.broadcast_to(target, (n, toks))).astype(F32)
    upper = (iota((toks, toks), 0) <= iota((toks, toks), 1)).astype(BF)
    cum = dot(hits.astype(BF), upper)
    rank = jnp.sum(cum * hits, axis=0, keepdims=True).astype(jnp.int32) - 1
    slot = target * share + rank
    onehot[...] = (iota((toks, toks), 0) == jnp.broadcast_to(slot, (toks, toks))).astype(F32).astype(BF)
    line = (within // IW).astype(F32)
    spot = (within - within // IW * IW).astype(F32)
    row_no = iota((128, toks), 0)
    places = jnp.where(row_no == HDIM, jnp.broadcast_to(spot, (128, toks)), 0.0)
    places = jnp.where(row_no == HDIM + 1, jnp.broadcast_to(line, (128, toks)), places)
    posout[...] = dot_nt(onehot[...], places.astype(BF))

    pair.wait()
    lanes = pl.ds(pl.multiple_of(core * half, 128), half)
    half_send[...] = (st_send[:, lanes].astype(F32) + pair_recv[:, lanes].astype(F32)).astype(BF)

    def chip_copy(to):
        return remote(
            half_send, half_recv.at[chip], hsend.at[to], hrecv.at[chip], 2 * to + core
        )

    for to in range(1, chips):

        @pl.when(chip < to)
        def _(to=to):
            chip_copy(to).start()

    lax.fori_loop(0, lo, project, 0)
    shift_in(qs, 0, True)

    heads_per = BLK // HDIM
    lane_head = iota((1, BLK), 1) // HDIM
    masks = []
    for c in range(2):
        sc = span_col[c * chunk : (c + 1) * chunk, :]
        sr = span_row[:, c * chunk : (c + 1) * chunk]
        keep = (sr <= sc) & (sc < lasts[c])
        masks.append(keep.astype(F32))
    allowed = (span_row <= span_col).astype(F32).astype(BF)

    def local(g, carry_in):
        cols = pl.ds(pl.multiple_of(g * BLK, BLK), BLK)
        kvis[:, cols] = dot(allowed, ks[:, cols])
        for c in range(2):
            rs = pl.ds(c * chunk, chunk)
            q8 = qs[rs, cols]
            k8 = ks[rs, cols]
            v8 = vs[rs, cols]
            acc = jnp.zeros((chunk, BLK), F32)
            for h in range(heads_per):
                hm = (lane_head == h).astype(F32).astype(BF)
                scores = (dot_nt(q8 * hm, k8) * masks[c]).astype(BF)
                acc = acc + dot(scores, v8 * hm)
            num[rs, cols] = acc
        return carry_in

    lax.fori_loop(0, groups, local, 0)

    fin_send[...] = jnp.zeros_like(fin_send)
    carry[:, lanes] = jnp.zeros((HDIM, half), F32)
    for src in range(chips - 1):

        @pl.when(src < chip)
        def _(src=src):
            remote(
                half_send, half_recv.at[src], hsend.at[src], hrecv.at[src], partner
            ).wait_recv()
            carry[:, lanes] = carry[:, lanes] + half_recv[src].astype(F32)

    fin_send[...] = carry[:, lanes].astype(BF)
    fin = remote(fin_send, fin_recv, fsem.at[0], fsem.at[1], partner)
    fin.start()
    after[...] = jnp.zeros_like(after)
    for k in range(2):

        @pl.when(me + 1 + k < n)
        def _(k=k):
            remote(
                lead_send, lead_recv.at[k], lead_ssem.at[k], lead_rsem.at[k], partner
            ).wait_recv()
            got = lead_recv[k].astype(F32)
            same = (got[HDIM - 1 : HDIM, pad - 128 : pad - 127] == last_seg).astype(F32)
            after[...] = after[...] + got * same

    fin.wait()
    other = pl.ds(pl.multiple_of((1 - core) * half, 128), half)
    carry[:, other] = fin_recv[...].astype(F32)

    @pl.when(core == 1)
    def _():
        carry[...] = carry[...] + pair_recv[...].astype(F32)

    reach = [(lasts[c] == last_seg).astype(F32) for c in range(2)]
    dev_tail = (span_col == last_seg).astype(F32)
    tails = [
        (span_col[c * chunk : (c + 1) * chunk, :] == lasts[c]).astype(F32) for c in range(2)
    ]
    ones_block = block_f.astype(BF)

    def spread(ref, g):
        per = BLK // 128
        rows = [ref[pl.ds(per * g + r, 1), pad - 128 :] for r in range(per)]
        return jnp.concatenate(rows, axis=1)

    for g in range(groups):
        cols = pl.ds(g * BLK, BLK)
        valid = iota((1, BLK), 1) + g * BLK < inner
        live = (iota((HDIM, BLK), 1) + g * BLK) < inner
        zero = jnp.zeros((HDIM, BLK), F32)
        car = jnp.where(live, carry[:, cols], zero)
        aft = jnp.where(live, after[:, cols], zero)
        if g * BLK + BLK <= (inner + 127) // 128 * 128:
            csum, asum = spread(carry, g), spread(after, g)
        else:
            need = (inner - g * BLK + 127) // 128
            csum = jnp.concatenate(
                [carry[2 * g + r : 2 * g + r + 1, pad - 128 :] if r < need
                 else jnp.zeros((1, 128), F32) for r in range(2)], axis=1)
            asum = jnp.concatenate(
                [after[2 * g + r : 2 * g + r + 1, pad - 128 :] if r < need
                 else jnp.zeros((1, 128), F32) for r in range(2)], axis=1)
        csum = jnp.where(valid, csum, 0.0)
        asum = jnp.where(valid, asum, 0.0)
        st_all = jnp.where(live, st_send[:, cols].astype(F32), zero)
        for c in range(2):
            rs = pl.ds(c * chunk, chunk)
            q8 = qs[rs, cols].astype(F32)
            q_tail = (q8 * tails[c]).astype(BF)
            q_non = (q8 * (1.0 - tails[c])).astype(BF)
            if c == 0:
                a_state = car
                b_state = st_b0[:, cols] + car + aft * reach[0]
            else:
                a_state = st_c0[:, cols] + car
                b_state = st_all + car + aft
            numer = num[rs, cols] + dot(q_non, expand(a_state)) + dot(q_tail, expand(b_state))
            seen = kvis[rs, cols] + csum + dev_tail[c * chunk : (c + 1) * chunk] * asum
            den = dot((q8 * seen).astype(BF), ones_block)
            att[rs, cols] = (numer / (1.0 + den)).astype(BF)

    ocopy.wait()
    xlat[...] = jnp.zeros_like(xlat)

    def tail_rows(r, c):
        rs = pl.ds(pl.multiple_of(r * BLK, BLK), BLK)
        mixed = hid[rs, :].astype(F32) + dot(att[rs, :inner], wo[...])
        meansq = jnp.sum(mixed * mixed, axis=1, keepdims=True) * (1.0 / d)
        normed = (mixed * lax.rsqrt(meansq + 1e-06) * gain[...]).astype(BF)
        lat = noisy[rs, :] - 0.5 * dot(normed, vw[...])
        lat_out[rs, :] = lat
        xlat[rs, 0:HDIM] = lat
        return c

    lax.fori_loop(0, toks // BLK, tail_rows, 0)

    outgoing[...] = (dot(onehot[...], xlat[...].astype(BF)) + posout[...]).astype(BF)

    def out_copy(k):
        to = lax.rem(me + k, n)
        return remote(
            outgoing.at[pl.ds(pl.multiple_of(to * share, share), share)],
            incoming.at[pl.ds(pl.multiple_of(me * share, share), share)],
            asend.at[k], arecv.at[me], to,
        )

    for k in range(1, n):
        out_copy(k).start()
    own = pl.ds(pl.multiple_of(me * share, share), share)
    incoming[own, :] = outgoing[own, :]
    for k in range(1, n):
        src = lax.rem(me + k, n)
        remote(
            outgoing.at[pl.ds(0, share)],
            incoming.at[pl.ds(pl.multiple_of(src * share, share), share)],
            asend.at[k], arecv.at[src], src,
        ).wait_recv()

    got = incoming[...]
    lane_no = iota((8, 128), 1)
    pick = jnp.where(lane_no == HDIM, 1.0, jnp.where(lane_no == HDIM + 1, float(IW), 0.0)).astype(BF)
    pos = dot_nt(pick, got)[0:1, :].astype(jnp.int32)
    onehot[...] = (iota((toks, toks), 0) == jnp.broadcast_to(pos, (toks, toks))).astype(F32).astype(BF)
    tile = dot(onehot[...], got)
    edge = 2 * IW
    wide[edge : edge + toks, :] = tile
    halo_send[0] = tile[:edge].astype(BF)
    halo_send[1] = tile[toks - edge :].astype(BF)

    def halo(k, to):
        return remote(halo_send.at[k], halo_recv.at[k], halo_ssem.at[k], halo_rsem.at[k], to)

    @pl.when(me > 0)
    def _():
        halo(0, me - 1).start()

    @pl.when(me < n - 1)
    def _():
        halo(1, me + 1).start()

    wide[0:edge, :] = jnp.zeros((edge, 128), F32)
    wide[edge + toks :, :] = jnp.zeros((edge, 128), F32)

    @pl.when(me > 0)
    def _():
        halo(1, partner).wait_recv()
        wide[0:edge, :] = halo_recv[1].astype(F32)

    @pl.when(me < n - 1)
    def _():
        halo(0, partner).wait_recv()
        wide[edge + toks :, :] = halo_recv[0].astype(F32)

    ext = toks + 2 * edge
    x = wide[...]
    column = lax.rem(iota((ext, 128), 0), IW)
    lane = iota((ext, 128), 1)
    left = jnp.where(column == 0, 0.0, pltpu.roll(x, 1, 0))
    right = jnp.where(column == IW - 1, 0.0, pltpu.roll(x, ext - 1, 0))
    three = jnp.where(
        lane < HDIM, left,
        jnp.where(lane < 2 * HDIM, pltpu.roll(x, HDIM, 1),
                  jnp.where(lane < 3 * HDIM, pltpu.roll(right, 2 * HDIM, 1), 0.0)),
    )
    three = three.astype(BF)
    mid = toks + 2 * IW
    k3 = 3 * HDIM
    acc = dot(three[0:mid, :k3], w1[0])
    acc = acc + dot(three[IW : IW + mid, :k3], w1[1])
    acc = acc + dot(three[2 * IW : 2 * IW + mid, :k3], w1[2])
    feat = acc / (1.0 + jnp.exp(-acc))
    row_at = iota((mid, 1), 0) // IW
    outside = ((row_at == 0) & (me == 0)) | ((row_at == mid // IW - 1) & (me == n - 1))
    feat = jnp.where(outside, 0.0, feat).astype(BF).astype(F32)
    column = lax.rem(iota((mid, 1), 0), IW)
    shifted[1] = feat.astype(BF)
    shifted[0] = jnp.where(column == 0, 0.0, pltpu.roll(feat, 1, 0)).astype(BF)
    shifted[2] = jnp.where(column == IW - 1, 0.0, pltpu.roll(feat, mid - 1, 0)).astype(BF)
    w2copy.wait()
    out = None
    for a in range(3):
        for b in range(3):
            part = dot(shifted[b, a * IW : a * IW + toks, :], w2[3 * a + b])
            out = part if out is None else out + part
    dec_out[...] = out.astype(BF)

    for k in range(2):

        @pl.when(me >= k + 1)
        def _(k=k):
            lead_copy(k).wait_send()

    for to in range(1, chips):

        @pl.when(chip < to)
        def _(to=to):
            chip_copy(to).wait_send()

    for k in range(1, n):
        out_copy(k).wait_send()

    @pl.when(me > 0)
    def _():
        halo(0, me - 1).wait_send()

    @pl.when(me < n - 1)
    def _():
        halo(1, me + 1).wait_send()


def body(
    hidden_in, noisy_latents, span_ids, tile_map, qkv_weight, out_weight,
    norm_gain, velocity_weight, conv_first, conv_second,
):
    toks, d = hidden_in.shape
    inner = out_weight.shape[0]
    n = lax.axis_size("span")
    pad = -(-(inner + 128) // BLK) * BLK
    ch = conv_first.shape[3]
    wide_cols = -(-qkv_weight.shape[1] // 128) * 128
    pack_cols = max(wide_cols, 2 * inner // 128 * 128 + pad + 128)
    chips = n // 2
    edge = 2 * IW
    mid = toks + 2 * IW
    blocks = -(-qkv_weight.shape[1] // BLK)
    vm, dma = pltpu.VMEM, pltpu.SemaphoreType.DMA
    any_, vmem = pl.BlockSpec(memory_space=pl.ANY), pl.BlockSpec(memory_space=pltpu.VMEM)
    scratch = [
        vm((toks, d), BF), vm(qkv_weight.shape, BF), vm(out_weight.shape, BF),
        vm((9, ch, ch), BF), vm((toks, pack_cols), BF),
        vm((toks, pad), BF), vm((toks, pad), BF), vm((toks, pad), BF),
        vm((toks, pad), F32), vm((toks, pad), F32), vm((toks, pad), BF),
        vm((HDIM, pad), F32), vm((HDIM, pad), F32),
        vm((HDIM, pad), BF), vm((HDIM, pad), BF), vm((HDIM, pad), BF), vm((2, HDIM, pad), BF),
        vm((HDIM, pad // 2), BF), vm((chips, HDIM, pad // 2), BF),
        vm((HDIM, pad // 2), BF), vm((HDIM, pad // 2), BF),
        vm((HDIM, pad), F32), vm((HDIM, pad), F32),
        vm((toks, toks), BF), vm((toks, 128), F32), vm((toks, 128), F32),
        vm((toks, 128), BF), vm((toks, 128), BF),
        vm((toks + 2 * edge, 128), F32), vm((2, edge, 128), BF), vm((2, edge, 128), BF),
        vm((8, 128), BF), vm((3, mid, ch), BF),
        dma((blocks,)), dma((3,)), dma((2,)), dma((chips,)), dma((chips,)), dma((2,)),
        dma((2,)), dma((2,)), dma((n,)), dma((n,)), dma((2,)), dma((2,)),
    ]
    latents, decoded = pl.pallas_call(
        functools.partial(kernel, (n, toks, d, inner, pad)),
        out_shape=(
            jax.ShapeDtypeStruct(noisy_latents.shape, F32),
            jax.ShapeDtypeStruct((toks, ch), BF),
        ),
        in_specs=[any_, vmem, vmem, vmem, any_, any_, vmem, vmem, vmem, any_],
        out_specs=(vmem, vmem),
        scratch_shapes=scratch,
        compiler_params=pltpu.CompilerParams(
            collective_id=0, has_side_effects=True, vmem_limit_bytes=60 * 1024 * 1024
        ),
    )(
        hidden_in, noisy_latents, span_ids.reshape(1, toks), tile_map.reshape(n, toks),
        qkv_weight, out_weight, norm_gain.reshape(1, d), velocity_weight,
        conv_first.reshape(3, 3 * HDIM, ch), conv_second.reshape(9, ch, ch),
    )
    return latents, decoded.reshape(toks // IW, IW, ch)


def solution(mesh):
    rows = P(("groups", "span"), None)
    placed = (rows, rows, P(("groups", "span")), P("groups")) + (P(),) * 6
    return jax.shard_map(
        body, mesh=mesh, in_specs=placed,
        out_specs=(rows, P(("groups", "span"), None, None)), check_vma=False,
    )
```

```python
import functools

import jax
import jax.numpy as jnp
from jax import lax
from jax.experimental import pallas as pl
from jax.experimental.pallas import tpu as pltpu
from jax.sharding import PartitionSpec as P

HDIM = 32
IW = 64
BLK = 256
BF = jnp.bfloat16
F32 = jnp.float32


def dot(a, b):
    return jnp.dot(a, b, preferred_element_type=F32)


def dot_nt(a, b):
    return lax.dot_general(a, b, (((1,), (1,)), ((), ())), preferred_element_type=F32)


def dot_tn(a, b):
    return lax.dot_general(a, b, (((0,), (0,)), ((), ())), preferred_element_type=F32)


def iota(shape, axis):
    return lax.broadcasted_iota(jnp.int32, shape, axis)


def kernel(
    cfg,
    hid_hbm, noisy, span_ref, map_ref, wq_hbm, wo_hbm, gain, vw, w1, w2_hbm,
    lat_out, dec_out,
    hidt, hid, wq, wo, w2, packed, qs, ks, vs, num, kvis, att,
    st_c0, st_b0, st_send, lead_send, pair_recv, lead_recv, half_send, half_recv,
    fin_send, fin_recv, carry, after, onehot, xlat, outgoing, incoming,
    wide, halo_send, halo_recv, first, shifted,
    wsem, lsem, psem, hsend, hrecv, fsem, lead_ssem, lead_rsem, asend, arecv, halo_ssem, halo_rsem,
):
    n, toks, d, inner, pad = cfg
    half = pad // 2
    chips = n // 2
    groups = pad // BLK
    me = lax.axis_index("span")
    core = lax.rem(me, 2)
    chip = me // 2
    partner = me + 1 - 2 * core
    share = toks // n
    chunk = toks // 2

    def remote(src, dst, ss, rs, dev):
        return pltpu.make_async_remote_copy(
            src_ref=src, dst_ref=dst, send_sem=ss, recv_sem=rs,
            device_id={"span": dev}, device_id_type=pl.DeviceIdType.MESH,
        )

    barrier = pltpu.get_barrier_semaphore()
    for k in range(1, n):
        pl.semaphore_signal(
            barrier, inc=1, device_id={"span": lax.rem(me + k, n)},
            device_id_type=pl.DeviceIdType.MESH,
        )

    total = wq_hbm.shape[1]
    full = total // BLK
    rest = total - full * BLK
    lo = inner // BLK

    def wcopy(b):
        cols = pl.ds(pl.multiple_of(b * BLK, BLK), BLK)
        return pltpu.make_async_copy(wq_hbm.at[:, cols], wq.at[:, cols], wsem.at[b])

    hcopy = pltpu.make_async_copy(hid_hbm, hidt, lsem.at[0])
    hcopy.start()
    for b in range(lo, full):
        wcopy(b).start()
    tail_copy = None
    if rest:
        tail_copy = pltpu.make_async_copy(
            wq_hbm.at[:, full * BLK : total], wq.at[:, full * BLK : total], wsem.at[full]
        )
        tail_copy.start()
    for b in range(lo):
        wcopy(b).start()
    ocopy = pltpu.make_async_copy(wo_hbm, wo, lsem.at[1])
    ocopy.start()
    w2copy = pltpu.make_async_copy(w2_hbm, w2, lsem.at[2])
    w2copy.start()

    span_row = span_ref[...].astype(F32)
    span_col = jnp.transpose(jnp.broadcast_to(span_row, (128, toks)))[:, 0:1]
    first_seg = span_col[0:1, :]
    last_seg = span_col[toks - 1 : toks, :]
    lasts = [span_col[(c + 1) * chunk - 1 : (c + 1) * chunk, :] for c in range(2)]

    hcopy.wait()

    def turn(i, c):
        cols = pl.ds(pl.multiple_of(i * 128, 128), 128)
        hid[cols, :] = jnp.transpose(hidt[:, cols])
        return c

    lax.fori_loop(0, toks // 128, turn, 0)

    def project(b, carry_in):
        wcopy(b).wait()
        cols = pl.ds(pl.multiple_of(b * BLK, BLK), BLK)
        packed[:, cols] = dot(hid[...], wq[:, cols]).astype(BF)
        return carry_in

    lax.fori_loop(lo, full, project, 0)
    if rest:
        tail_copy.wait()
        packed[:, full * BLK : total] = dot(hid[...], wq[:, full * BLK : total]).astype(BF)

    def shift_in(dst, begin, relu):
        base = begin // 128 * 128
        off = begin - base
        width = packed.shape[1]
        end = min(base + pad + 128, width)

        def rows(r, c):
            rs = pl.ds(pl.multiple_of(r * 128, 128), 128)
            val = packed[rs, base:end].astype(F32)
            if off:
                val = pltpu.roll(val, val.shape[1] - off, 1)
            val = val[:, :pad]
            if relu:
                val = jnp.maximum(val, 0.0)
            val = jnp.where(iota((128, pad), 1) < inner, val, 0.0)
            dst[rs, :] = val.astype(BF)
            return c

        lax.fori_loop(0, toks // 128, rows, 0)

    shift_in(ks, inner, True)
    shift_in(vs, 2 * inner, False)

    block = (iota((BLK, BLK), 0) // HDIM == iota((BLK, BLK), 1) // HDIM)
    block_f = block.astype(F32)

    def compact(full_state):
        kept = jnp.where(block, full_state, 0.0)
        out = kept[0:HDIM]
        for h in range(1, BLK // HDIM):
            out = out + kept[h * HDIM : (h + 1) * HDIM]
        return out

    def expand(small):
        return (jnp.concatenate([small] * (BLK // HDIM), axis=0) * block_f).astype(BF)

    lead_col = (span_col == first_seg).astype(F32)
    to_b0 = (span_col[chunk:, :] <= lasts[0]).astype(F32)

    def states(g, c):
        cols = pl.ds(pl.multiple_of(g * BLK, BLK), BLK)
        k8 = ks[:, cols]
        v8 = vs[:, cols]
        s0 = compact(dot_tn(k8[:chunk], v8[:chunk]))
        s1 = compact(dot_tn(k8[chunk:], v8[chunk:]))
        k1 = (k8[chunk:].astype(F32) * to_b0).astype(BF)
        sb = compact(dot_tn(k1, v8[chunk:]))
        kl = (k8.astype(F32) * lead_col).astype(BF)
        sl = compact(dot_tn(kl, v8))
        st_c0[:, cols] = s0
        st_b0[:, cols] = s0 + sb
        num[0:HDIM, cols] = s0 + s1
        num[HDIM : 2 * HDIM, cols] = sl
        return c

    lax.fori_loop(0, groups, states, 0)

    def pack_sums(dst, column):
        kf = ks[...].astype(F32)
        if column is not None:
            kf = kf * column
        sums = jnp.sum(kf, axis=0, keepdims=True)
        parts = [sums[:, 128 * r : 128 * (r + 1)] for r in range((inner + 127) // 128)]
        base_rows = jnp.zeros((HDIM, 128), F32)
        row_no = iota((HDIM, 128), 0)
        for r, part in enumerate(parts):
            base_rows = jnp.where(row_no == r, jnp.broadcast_to(part, (HDIM, 128)), base_rows)
        base_rows = jnp.where(
            row_no == HDIM - 1, jnp.broadcast_to(first_seg, (HDIM, 128)), base_rows
        )
        dst[:, pad - 128 :] = base_rows.astype(BF)

    st_send[:, : pad - 128] = num[0:HDIM, : pad - 128].astype(BF)
    lead_send[:, : pad - 128] = num[HDIM : 2 * HDIM, : pad - 128].astype(BF)
    pack_sums(st_send, None)
    pack_sums(lead_send, lead_col)

    pl.semaphore_wait(barrier, n - 1)
    pair = remote(st_send, pair_recv, psem.at[0], psem.at[1], partner)
    pair.start()

    def lead_copy(k):
        return remote(
            lead_send, lead_recv.at[k], lead_ssem.at[k], lead_rsem.at[k],
            lax.rem(me - 1 - k + n, n),
        )

    for k in range(2):

        @pl.when(me >= k + 1)
        def _(k=k):
            lead_copy(k).start()

    mine = map_ref[:, pl.ds(pl.multiple_of(me * toks, toks), toks)]
    target = mine // toks
    within = mine - target * toks
    hits = (iota((n, toks), 0) == jnp.broadcast_to(target, (n, toks))).astype(F32)
    upper = (iota((toks, toks), 0) <= iota((toks, toks), 1)).astype(BF)
    cum = dot(hits.astype(BF), upper)
    rank = jnp.sum(cum * hits, axis=0, keepdims=True).astype(jnp.int32) - 1
    slot = target * share + rank
    onehot[...] = (iota((toks, toks), 0) == jnp.broadcast_to(slot, (toks, toks))).astype(F32).astype(BF)
    line = (within // IW).astype(F32)
    spot = (within - within // IW * IW).astype(F32)
    row_no = iota((128, toks), 0)
    places = jnp.where(row_no == HDIM, jnp.broadcast_to(spot, (128, toks)), 0.0)
    places = jnp.where(row_no == HDIM + 1, jnp.broadcast_to(line, (128, toks)), places)
    xlat[...] = places

    pair.wait()
    lanes = pl.ds(pl.multiple_of(core * half, 128), half)
    half_send[...] = (st_send[:, lanes].astype(F32) + pair_recv[:, lanes].astype(F32)).astype(BF)

    def chip_copy(to):
        return remote(
            half_send, half_recv.at[chip], hsend.at[to], hrecv.at[chip], 2 * to + core
        )

    for to in range(1, chips):

        @pl.when(chip < to)
        def _(to=to):
            chip_copy(to).start()

    lax.fori_loop(0, lo, project, 0)
    shift_in(qs, 0, True)

    heads_per = BLK // HDIM
    lane_head = iota((1, BLK), 1) // HDIM
    masks = []
    for c in range(2):
        sc = span_col[c * chunk : (c + 1) * chunk, :]
        sr = span_row[:, c * chunk : (c + 1) * chunk]
        keep = (sr <= sc) & (sc < lasts[c])
        masks.append(keep.astype(F32))
    allowed = (span_row <= span_col).astype(F32).astype(BF)

    def local(g, carry_in):
        cols = pl.ds(pl.multiple_of(g * BLK, BLK), BLK)
        kvis[:, cols] = dot(allowed, ks[:, cols])
        for c in range(2):
            rs = pl.ds(c * chunk, chunk)
            q8 = qs[rs, cols]
            k8 = ks[rs, cols]
            v8 = vs[rs, cols]
            acc = jnp.zeros((chunk, BLK), F32)
            for h in range(heads_per):
                hm = (lane_head == h).astype(F32).astype(BF)
                scores = (dot_nt(q8 * hm, k8) * masks[c]).astype(BF)
                acc = acc + dot(scores, v8 * hm)
            num[rs, cols] = acc
        return carry_in

    lax.fori_loop(0, groups, local, 0)

    fin_send[...] = jnp.zeros_like(fin_send)
    carry[:, lanes] = jnp.zeros((HDIM, half), F32)
    for src in range(chips - 1):

        @pl.when(src < chip)
        def _(src=src):
            remote(
                half_send, half_recv.at[src], hsend.at[src], hrecv.at[src], partner
            ).wait_recv()
            carry[:, lanes] = carry[:, lanes] + half_recv[src].astype(F32)

    fin_send[...] = carry[:, lanes].astype(BF)
    fin = remote(fin_send, fin_recv, fsem.at[0], fsem.at[1], partner)
    fin.start()
    after[...] = jnp.zeros_like(after)
    for k in range(2):

        @pl.when(me + 1 + k < n)
        def _(k=k):
            remote(
                lead_send, lead_recv.at[k], lead_ssem.at[k], lead_rsem.at[k], partner
            ).wait_recv()
            got = lead_recv[k].astype(F32)
            same = (got[HDIM - 1 : HDIM, pad - 128 : pad - 127] == last_seg).astype(F32)
            after[...] = after[...] + got * same

    fin.wait()
    other = pl.ds(pl.multiple_of((1 - core) * half, 128), half)
    carry[:, other] = fin_recv[...].astype(F32)

    @pl.when(core == 1)
    def _():
        carry[...] = carry[...] + pair_recv[...].astype(F32)

    reach = [(lasts[c] == last_seg).astype(F32) for c in range(2)]
    dev_tail = (span_col == last_seg).astype(F32)
    tails = [
        (span_col[c * chunk : (c + 1) * chunk, :] == lasts[c]).astype(F32) for c in range(2)
    ]
    ones_block = block_f.astype(BF)

    def spread(ref, g):
        per = BLK // 128
        rows = [ref[pl.ds(per * g + r, 1), pad - 128 :] for r in range(per)]
        return jnp.concatenate(rows, axis=1)

    for g in range(groups):
        cols = pl.ds(g * BLK, BLK)
        valid = iota((1, BLK), 1) + g * BLK < inner
        live = (iota((HDIM, BLK), 1) + g * BLK) < inner
        zero = jnp.zeros((HDIM, BLK), F32)
        car = jnp.where(live, carry[:, cols], zero)
        aft = jnp.where(live, after[:, cols], zero)
        if g * BLK + BLK <= (inner + 127) // 128 * 128:
            csum, asum = spread(carry, g), spread(after, g)
        else:
            need = (inner - g * BLK + 127) // 128
            csum = jnp.concatenate(
                [carry[2 * g + r : 2 * g + r + 1, pad - 128 :] if r < need
                 else jnp.zeros((1, 128), F32) for r in range(2)], axis=1)
            asum = jnp.concatenate(
                [after[2 * g + r : 2 * g + r + 1, pad - 128 :] if r < need
                 else jnp.zeros((1, 128), F32) for r in range(2)], axis=1)
        csum = jnp.where(valid, csum, 0.0)
        asum = jnp.where(valid, asum, 0.0)
        st_all = jnp.where(live, st_send[:, cols].astype(F32), zero)
        for c in range(2):
            rs = pl.ds(c * chunk, chunk)
            q8 = qs[rs, cols].astype(F32)
            q_tail = (q8 * tails[c]).astype(BF)
            q_non = (q8 * (1.0 - tails[c])).astype(BF)
            if c == 0:
                a_state = car
                b_state = st_b0[:, cols] + car + aft * reach[0]
            else:
                a_state = st_c0[:, cols] + car
                b_state = st_all + car + aft
            numer = num[rs, cols] + dot(q_non, expand(a_state)) + dot(q_tail, expand(b_state))
            seen = kvis[rs, cols] + csum + dev_tail[c * chunk : (c + 1) * chunk] * asum
            den = dot((q8 * seen).astype(BF), ones_block)
            att[rs, cols] = (numer / (1.0 + den)).astype(BF)

    ocopy.wait()

    def tail_rows(r, c):
        rs = pl.ds(pl.multiple_of(r * BLK, BLK), BLK)
        mixed = hid[rs, :].astype(F32) + dot(att[rs, :inner], wo[...])
        meansq = jnp.sum(mixed * mixed, axis=1, keepdims=True) * (1.0 / d)
        normed = (mixed * lax.rsqrt(meansq + 1e-06) * jnp.broadcast_to(gain[...][None, :], (BLK, d))).astype(BF)
        lat = noisy[:, rs] - 0.5 * dot_nt(vw[...], normed)
        lat_out[:, rs] = lat
        xlat[0:HDIM, rs] = lat
        return c

    lax.fori_loop(0, toks // BLK, tail_rows, 0)

    outgoing[...] = dot_nt(onehot[...], xlat[...].astype(BF)).astype(BF)

    def out_copy(k):
        to = lax.rem(me + k, n)
        return remote(
            outgoing.at[pl.ds(pl.multiple_of(to * share, share), share)],
            incoming.at[pl.ds(pl.multiple_of(me * share, share), share)],
            asend.at[k], arecv.at[me], to,
        )

    for k in range(1, n):
        out_copy(k).start()
    own = pl.ds(pl.multiple_of(me * share, share), share)
    incoming[own, :] = outgoing[own, :]
    for k in range(1, n):
        src = lax.rem(me + k, n)
        remote(
            outgoing.at[pl.ds(0, share)],
            incoming.at[pl.ds(pl.multiple_of(src * share, share), share)],
            asend.at[k], arecv.at[src], src,
        ).wait_recv()

    got = incoming[...]
    lane_no = iota((8, 128), 1)
    pick = jnp.where(lane_no == HDIM, 1.0, jnp.where(lane_no == HDIM + 1, float(IW), 0.0)).astype(BF)
    pos = dot_nt(pick, got)[0:1, :].astype(jnp.int32)
    onehot[...] = (iota((toks, toks), 0) == jnp.broadcast_to(pos, (toks, toks))).astype(F32).astype(BF)
    tile = dot(onehot[...], got)
    edge = 2 * IW
    wide[edge : edge + toks, :] = tile
    halo_send[0] = tile[:edge].astype(BF)
    halo_send[1] = tile[toks - edge :].astype(BF)

    def halo(k, to):
        return remote(halo_send.at[k], halo_recv.at[k], halo_ssem.at[k], halo_rsem.at[k], to)

    @pl.when(me > 0)
    def _():
        halo(0, me - 1).start()

    @pl.when(me < n - 1)
    def _():
        halo(1, me + 1).start()

    wide[0:edge, :] = jnp.zeros((edge, 128), F32)
    wide[edge + toks :, :] = jnp.zeros((edge, 128), F32)

    @pl.when(me > 0)
    def _():
        halo(1, partner).wait_recv()
        wide[0:edge, :] = halo_recv[1].astype(F32)

    @pl.when(me < n - 1)
    def _():
        halo(0, partner).wait_recv()
        wide[edge + toks :, :] = halo_recv[0].astype(F32)

    ext = toks + 2 * edge
    x = wide[...]
    column = lax.rem(iota((ext, 128), 0), IW)
    lane = iota((ext, 128), 1)
    left = jnp.where(column == 0, 0.0, pltpu.roll(x, 1, 0))
    right = jnp.where(column == IW - 1, 0.0, pltpu.roll(x, ext - 1, 0))
    three = jnp.where(
        lane < HDIM, left,
        jnp.where(lane < 2 * HDIM, pltpu.roll(x, HDIM, 1),
                  jnp.where(lane < 3 * HDIM, pltpu.roll(right, 2 * HDIM, 1), 0.0)),
    )
    three = three.astype(BF)
    mid = toks + 2 * IW
    k3 = 3 * HDIM
    acc = dot(three[0:mid, :k3], w1[0])
    acc = acc + dot(three[IW : IW + mid, :k3], w1[1])
    acc = acc + dot(three[2 * IW : 2 * IW + mid, :k3], w1[2])
    feat = acc / (1.0 + jnp.exp(-acc))
    row_at = iota((mid, 1), 0) // IW
    outside = ((row_at == 0) & (me == 0)) | ((row_at == mid // IW - 1) & (me == n - 1))
    feat = jnp.where(outside, 0.0, feat).astype(BF).astype(F32)
    column = lax.rem(iota((mid, 1), 0), IW)
    shifted[1] = feat.astype(BF)
    shifted[0] = jnp.where(column == 0, 0.0, pltpu.roll(feat, 1, 0)).astype(BF)
    shifted[2] = jnp.where(column == IW - 1, 0.0, pltpu.roll(feat, mid - 1, 0)).astype(BF)
    w2copy.wait()
    out = None
    for a in range(3):
        for b in range(3):
            part = dot(shifted[b, a * IW : a * IW + toks, :], w2[3 * a + b])
            out = part if out is None else out + part
    dec_out[...] = out.astype(BF)

    for k in range(2):

        @pl.when(me >= k + 1)
        def _(k=k):
            lead_copy(k).wait_send()

    for to in range(1, chips):

        @pl.when(chip < to)
        def _(to=to):
            chip_copy(to).wait_send()

    for k in range(1, n):
        out_copy(k).wait_send()

    @pl.when(me > 0)
    def _():
        halo(0, me - 1).wait_send()

    @pl.when(me < n - 1)
    def _():
        halo(1, me + 1).wait_send()


def body(
    hidden_in, noisy_latents, span_ids, tile_map, qkv_weight, out_weight,
    norm_gain, velocity_weight, conv_first, conv_second,
):
    toks, d = hidden_in.shape
    inner = out_weight.shape[0]
    n = lax.axis_size("span")
    pad = -(-(inner + 128) // BLK) * BLK
    ch = conv_first.shape[3]
    wide_cols = -(-qkv_weight.shape[1] // 128) * 128
    pack_cols = max(wide_cols, 2 * inner // 128 * 128 + pad + 128)
    chips = n // 2
    edge = 2 * IW
    mid = toks + 2 * IW
    blocks = -(-qkv_weight.shape[1] // BLK)
    vm, dma = pltpu.VMEM, pltpu.SemaphoreType.DMA
    any_, vmem = pl.BlockSpec(memory_space=pl.ANY), pl.BlockSpec(memory_space=pltpu.VMEM)
    scratch = [
        vm((d, toks), BF), vm((toks, d), BF), vm(qkv_weight.shape, BF), vm(out_weight.shape, BF),
        vm((9, ch, ch), BF), vm((toks, pack_cols), BF),
        vm((toks, pad), BF), vm((toks, pad), BF), vm((toks, pad), BF),
        vm((toks, pad), F32), vm((toks, pad), F32), vm((toks, pad), BF),
        vm((HDIM, pad), F32), vm((HDIM, pad), F32),
        vm((HDIM, pad), BF), vm((HDIM, pad), BF), vm((HDIM, pad), BF), vm((2, HDIM, pad), BF),
        vm((HDIM, pad // 2), BF), vm((chips, HDIM, pad // 2), BF),
        vm((HDIM, pad // 2), BF), vm((HDIM, pad // 2), BF),
        vm((HDIM, pad), F32), vm((HDIM, pad), F32),
        vm((toks, toks), BF), vm((128, toks), F32),
        vm((toks, 128), BF), vm((toks, 128), BF),
        vm((toks + 2 * edge, 128), F32), vm((2, edge, 128), BF), vm((2, edge, 128), BF),
        vm((8, 128), BF), vm((3, mid, ch), BF),
        dma((blocks,)), dma((3,)), dma((2,)), dma((chips,)), dma((chips,)), dma((2,)),
        dma((2,)), dma((2,)), dma((n,)), dma((n,)), dma((2,)), dma((2,)),
    ]
    latents, decoded = pl.pallas_call(
        functools.partial(kernel, (n, toks, d, inner, pad)),
        out_shape=(
            jax.ShapeDtypeStruct(noisy_latents.shape[::-1], F32),
            jax.ShapeDtypeStruct((toks, ch), BF),
        ),
        in_specs=[any_, vmem, vmem, vmem, any_, any_, vmem, vmem, vmem, any_],
        out_specs=(vmem, vmem),
        scratch_shapes=scratch,
        compiler_params=pltpu.CompilerParams(
            collective_id=0, has_side_effects=True, vmem_limit_bytes=60 * 1024 * 1024
        ),
    )(
        hidden_in.T, noisy_latents.T, span_ids.reshape(1, toks), tile_map.reshape(1, -1),
        qkv_weight, out_weight, norm_gain, velocity_weight.T,
        conv_first.reshape(3, 3 * HDIM, ch), conv_second.reshape(9, ch, ch),
    )
    return latents.T, decoded.reshape(toks // IW, IW, ch)


def solution(mesh):
    rows = P(("groups", "span"), None)
    placed = (rows, rows, P(("groups", "span")), P("groups")) + (P(),) * 6
    return jax.shard_map(
        body, mesh=mesh, in_specs=placed,
        out_specs=(rows, P(("groups", "span"), None, None)), check_vma=False,
    )
```

```python
import functools

import jax
import jax.numpy as jnp
from jax import lax
from jax.experimental import pallas as pl
from jax.experimental.pallas import tpu as pltpu
from jax.sharding import PartitionSpec as P

HDIM = 32
IW = 64
BLK = 256
BF = jnp.bfloat16
F32 = jnp.float32


def dot(a, b):
    return jnp.dot(a, b, preferred_element_type=F32)


def dot_nt(a, b):
    return lax.dot_general(a, b, (((1,), (1,)), ((), ())), preferred_element_type=F32)


def dot_tn(a, b):
    return lax.dot_general(a, b, (((0,), (0,)), ((), ())), preferred_element_type=F32)


def iota(shape, axis):
    return lax.broadcasted_iota(jnp.int32, shape, axis)


def kernel(
    cfg,
    hid_hbm, noisy, span_ref, map_ref, wq_hbm, wo_hbm, gain, vw, w1, w2_hbm,
    lat_out, dec_out,
    hidt, hid, wq, wo, w2, packed, qs, ks, vs, num, kvis, att,
    st_c0, st_b0, st_send, lead_send, pair_recv, lead_recv, half_send, half_recv,
    fin_send, fin_recv, carry, after, onehot, xlat, outgoing, incoming,
    wide, halo_send, halo_recv, first, shifted,
    wsem, lsem, psem, hsend, hrecv, fsem, lead_ssem, lead_rsem, asend, arecv, halo_ssem, halo_rsem,
):
    n, toks, d, inner, pad = cfg
    half = pad // 2
    chips = n // 2
    groups = pad // BLK
    me = lax.axis_index("span")
    core = lax.rem(me, 2)
    chip = me // 2
    partner = me + 1 - 2 * core
    share = toks // n
    chunk = toks // 2

    def remote(src, dst, ss, rs, dev):
        return pltpu.make_async_remote_copy(
            src_ref=src, dst_ref=dst, send_sem=ss, recv_sem=rs,
            device_id={"span": dev}, device_id_type=pl.DeviceIdType.MESH,
        )

    barrier = pltpu.get_barrier_semaphore()
    for k in range(1, n):
        pl.semaphore_signal(
            barrier, inc=1, device_id={"span": lax.rem(me + k, n)},
            device_id_type=pl.DeviceIdType.MESH,
        )

    total = wq_hbm.shape[1]
    full = total // BLK
    rest = total - full * BLK
    lo = inner // BLK

    def wcopy(b):
        cols = pl.ds(pl.multiple_of(b * BLK, BLK), BLK)
        return pltpu.make_async_copy(wq_hbm.at[:, cols], wq.at[:, cols], wsem.at[b])

    hcopy = pltpu.make_async_copy(hid_hbm, hidt, lsem.at[0])
    hcopy.start()
    for b in range(lo, full):
        wcopy(b).start()
    tail_copy = None
    if rest:
        tail_copy = pltpu.make_async_copy(
            wq_hbm.at[:, full * BLK : total], wq.at[:, full * BLK : total], wsem.at[full]
        )
        tail_copy.start()
    for b in range(lo):
        wcopy(b).start()
    ocopy = pltpu.make_async_copy(wo_hbm, wo, lsem.at[1])
    ocopy.start()
    w2copy = pltpu.make_async_copy(w2_hbm, w2, lsem.at[2])
    w2copy.start()

    span_row = span_ref[...].astype(F32)
    span_col = jnp.transpose(jnp.broadcast_to(span_row, (128, toks)))[:, 0:1]
    first_seg = span_col[0:1, :]
    last_seg = span_col[toks - 1 : toks, :]
    lasts = [span_col[(c + 1) * chunk - 1 : (c + 1) * chunk, :] for c in range(2)]

    hcopy.wait()

    def turn(i, c):
        cols = pl.ds(pl.multiple_of(i * 128, 128), 128)
        hid[cols, :] = jnp.transpose(hidt[:, cols])
        return c

    lax.fori_loop(0, toks // 128, turn, 0)

    def project(b, carry_in):
        wcopy(b).wait()
        cols = pl.ds(pl.multiple_of(b * BLK, BLK), BLK)
        packed[:, cols] = dot(hid[...], wq[:, cols]).astype(BF)
        return carry_in

    lax.fori_loop(lo, full, project, 0)
    if rest:
        tail_copy.wait()
        packed[:, full * BLK : total] = dot(hid[...], wq[:, full * BLK : total]).astype(BF)

    def shift_in(dst, begin, relu):
        base = begin // 128 * 128
        off = begin - base
        width = packed.shape[1]
        end = min(base + pad + 128, width)

        def rows(r, c):
            rs = pl.ds(pl.multiple_of(r * 128, 128), 128)
            val = packed[rs, base:end].astype(F32)
            if off:
                val = pltpu.roll(val, val.shape[1] - off, 1)
            val = val[:, :pad]
            if relu:
                val = jnp.maximum(val, 0.0)
            val = jnp.where(iota((128, pad), 1) < inner, val, 0.0)
            dst[rs, :] = val.astype(BF)
            return c

        lax.fori_loop(0, toks // 128, rows, 0)

    shift_in(ks, inner, True)
    shift_in(vs, 2 * inner, False)

    block = (iota((BLK, BLK), 0) // HDIM == iota((BLK, BLK), 1) // HDIM)
    block_f = block.astype(F32)

    def compact(full_state):
        kept = jnp.where(block, full_state, 0.0)
        out = kept[0:HDIM]
        for h in range(1, BLK // HDIM):
            out = out + kept[h * HDIM : (h + 1) * HDIM]
        return out

    def expand(small):
        return (jnp.concatenate([small] * (BLK // HDIM), axis=0) * block_f).astype(BF)

    lead_col = (span_col == first_seg).astype(F32)
    to_b0 = (span_col[chunk:, :] <= lasts[0]).astype(F32)

    def states(g, c):
        cols = pl.ds(pl.multiple_of(g * BLK, BLK), BLK)
        k8 = ks[:, cols]
        v8 = vs[:, cols]
        s0 = compact(dot_tn(k8[:chunk], v8[:chunk]))
        s1 = compact(dot_tn(k8[chunk:], v8[chunk:]))
        k1 = (k8[chunk:].astype(F32) * to_b0).astype(BF)
        sb = compact(dot_tn(k1, v8[chunk:]))
        kl = (k8.astype(F32) * lead_col).astype(BF)
        sl = compact(dot_tn(kl, v8))
        st_c0[:, cols] = s0
        st_b0[:, cols] = s0 + sb
        num[0:HDIM, cols] = s0 + s1
        num[HDIM : 2 * HDIM, cols] = sl
        return c

    lax.fori_loop(0, groups, states, 0)

    def pack_sums(dst, column):
        kf = ks[...].astype(F32)
        if column is not None:
            kf = kf * column
        sums = jnp.sum(kf, axis=0, keepdims=True)
        parts = [sums[:, 128 * r : 128 * (r + 1)] for r in range((inner + 127) // 128)]
        base_rows = jnp.zeros((HDIM, 128), F32)
        row_no = iota((HDIM, 128), 0)
        for r, part in enumerate(parts):
            base_rows = jnp.where(row_no == r, jnp.broadcast_to(part, (HDIM, 128)), base_rows)
        base_rows = jnp.where(
            row_no == HDIM - 1, jnp.broadcast_to(first_seg, (HDIM, 128)), base_rows
        )
        dst[:, pad - 128 :] = base_rows.astype(BF)

    st_send[:, : pad - 128] = num[0:HDIM, : pad - 128].astype(BF)
    lead_send[:, : pad - 128] = num[HDIM : 2 * HDIM, : pad - 128].astype(BF)
    pack_sums(st_send, None)
    pack_sums(lead_send, lead_col)

    pl.semaphore_wait(barrier, n - 1)
    pair = remote(st_send, pair_recv, psem.at[0], psem.at[1], partner)
    pair.start()

    def lead_copy(k):
        return remote(
            lead_send, lead_recv.at[k], lead_ssem.at[k], lead_rsem.at[k],
            lax.rem(me - 1 - k + n, n),
        )

    for k in range(2):

        @pl.when(me >= k + 1)
        def _(k=k):
            lead_copy(k).start()

    mine = map_ref[:, pl.ds(pl.multiple_of(me * toks, toks), toks)]
    target = mine // toks
    within = mine - target * toks
    hits = (iota((n, toks), 0) == jnp.broadcast_to(target, (n, toks))).astype(F32)
    upper = (iota((toks, toks), 0) <= iota((toks, toks), 1)).astype(BF)
    cum = dot(hits.astype(BF), upper)
    rank = jnp.sum(cum * hits, axis=0, keepdims=True).astype(jnp.int32) - 1
    slot = target * share + rank
    onehot[...] = (iota((toks, toks), 0) == jnp.broadcast_to(slot, (toks, toks))).astype(F32).astype(BF)
    line = (within // IW).astype(F32)
    spot = (within - within // IW * IW).astype(F32)
    row_no = iota((128, toks), 0)
    places = jnp.where(row_no == HDIM, jnp.broadcast_to(spot, (128, toks)), 0.0)
    places = jnp.where(row_no == HDIM + 1, jnp.broadcast_to(line, (128, toks)), places)
    xlat[...] = places

    pair.wait()
    lanes = pl.ds(pl.multiple_of(core * half, 128), half)
    half_send[...] = (st_send[:, lanes].astype(F32) + pair_recv[:, lanes].astype(F32)).astype(BF)

    def chip_copy(to):
        return remote(
            half_send, half_recv.at[chip], hsend.at[to], hrecv.at[chip], 2 * to + core
        )

    for to in range(1, chips):

        @pl.when(chip < to)
        def _(to=to):
            chip_copy(to).start()

    lax.fori_loop(0, lo, project, 0)
    shift_in(qs, 0, True)

    heads_per = BLK // HDIM
    lane_head = iota((1, BLK), 1) // HDIM
    masks = []
    for c in range(2):
        sc = span_col[c * chunk : (c + 1) * chunk, :]
        sr = span_row[:, c * chunk : (c + 1) * chunk]
        keep = (sr <= sc) & (sc < lasts[c])
        masks.append(keep.astype(F32))
    allowed = (span_row <= span_col).astype(F32).astype(BF)

    def local(g, heads):
        cols = pl.ds(g * BLK if isinstance(g, int) else pl.multiple_of(g * BLK, BLK), BLK)
        kvis[:, cols] = dot(allowed, ks[:, cols])
        for c in range(2):
            rs = pl.ds(c * chunk, chunk)
            q8 = qs[rs, cols]
            k8 = ks[rs, cols]
            v8 = vs[rs, cols]
            acc = None
            for h0 in range(0, heads, 2):
                parts = []
                vals = []
                for h in range(h0, min(h0 + 2, heads)):
                    hm = (lane_head == h).astype(F32).astype(BF)
                    parts.append((dot_nt(q8 * hm, k8) * masks[c]).astype(BF))
                    vals.append(v8 * hm)
                one = dot(jnp.concatenate(parts, axis=1), jnp.concatenate(vals, axis=0))
                acc = one if acc is None else acc + one
            num[rs, cols] = acc

    whole = inner // BLK

    def local_loop(g, carry_in):
        local(g, heads_per)
        return carry_in

    lax.fori_loop(0, whole, local_loop, 0)
    if inner > whole * BLK:
        local(whole, (inner - whole * BLK) // HDIM)

    fin_send[...] = jnp.zeros_like(fin_send)
    carry[:, lanes] = jnp.zeros((HDIM, half), F32)
    for src in range(chips - 1):

        @pl.when(src < chip)
        def _(src=src):
            remote(
                half_send, half_recv.at[src], hsend.at[src], hrecv.at[src], partner
            ).wait_recv()
            carry[:, lanes] = carry[:, lanes] + half_recv[src].astype(F32)

    fin_send[...] = carry[:, lanes].astype(BF)
    fin = remote(fin_send, fin_recv, fsem.at[0], fsem.at[1], partner)
    fin.start()
    after[...] = jnp.zeros_like(after)
    for k in range(2):

        @pl.when(me + 1 + k < n)
        def _(k=k):
            remote(
                lead_send, lead_recv.at[k], lead_ssem.at[k], lead_rsem.at[k], partner
            ).wait_recv()
            got = lead_recv[k].astype(F32)
            same = (got[HDIM - 1 : HDIM, pad - 128 : pad - 127] == last_seg).astype(F32)
            after[...] = after[...] + got * same

    fin.wait()
    other = pl.ds(pl.multiple_of((1 - core) * half, 128), half)
    carry[:, other] = fin_recv[...].astype(F32)

    @pl.when(core == 1)
    def _():
        carry[...] = carry[...] + pair_recv[...].astype(F32)

    reach = [(lasts[c] == last_seg).astype(F32) for c in range(2)]
    dev_tail = (span_col == last_seg).astype(F32)
    tails = [
        (span_col[c * chunk : (c + 1) * chunk, :] == lasts[c]).astype(F32) for c in range(2)
    ]
    ones_block = block_f.astype(BF)

    def spread(ref, g):
        per = BLK // 128
        rows = [ref[pl.ds(per * g + r, 1), pad - 128 :] for r in range(per)]
        return jnp.concatenate(rows, axis=1)

    for g in range(groups):
        cols = pl.ds(g * BLK, BLK)
        valid = iota((1, BLK), 1) + g * BLK < inner
        live = (iota((HDIM, BLK), 1) + g * BLK) < inner
        zero = jnp.zeros((HDIM, BLK), F32)
        car = jnp.where(live, carry[:, cols], zero)
        aft = jnp.where(live, after[:, cols], zero)
        if g * BLK + BLK <= (inner + 127) // 128 * 128:
            csum, asum = spread(carry, g), spread(after, g)
        else:
            need = (inner - g * BLK + 127) // 128
            csum = jnp.concatenate(
                [carry[2 * g + r : 2 * g + r + 1, pad - 128 :] if r < need
                 else jnp.zeros((1, 128), F32) for r in range(2)], axis=1)
            asum = jnp.concatenate(
                [after[2 * g + r : 2 * g + r + 1, pad - 128 :] if r < need
                 else jnp.zeros((1, 128), F32) for r in range(2)], axis=1)
        csum = jnp.where(valid, csum, 0.0)
        asum = jnp.where(valid, asum, 0.0)
        st_all = jnp.where(live, st_send[:, cols].astype(F32), zero)
        for c in range(2):
            rs = pl.ds(c * chunk, chunk)
            q8 = qs[rs, cols].astype(F32)
            q_tail = (q8 * tails[c]).astype(BF)
            q_non = (q8 * (1.0 - tails[c])).astype(BF)
            if c == 0:
                a_state = car
                b_state = st_b0[:, cols] + car + aft * reach[0]
            else:
                a_state = st_c0[:, cols] + car
                b_state = st_all + car + aft
            numer = num[rs, cols] + dot(q_non, expand(a_state)) + dot(q_tail, expand(b_state))
            seen = kvis[rs, cols] + csum + dev_tail[c * chunk : (c + 1) * chunk] * asum
            den = dot((q8 * seen).astype(BF), ones_block)
            att[rs, cols] = (numer / (1.0 + den)).astype(BF)

    ocopy.wait()

    def tail_rows(r, c):
        rs = pl.ds(pl.multiple_of(r * BLK, BLK), BLK)
        mixed = hid[rs, :].astype(F32) + dot(att[rs, :inner], wo[...])
        meansq = jnp.sum(mixed * mixed, axis=1, keepdims=True) * (1.0 / d)
        normed = (mixed * lax.rsqrt(meansq + 1e-06) * jnp.broadcast_to(gain[...][None, :], (BLK, d))).astype(BF)
        lat = noisy[:, rs] - 0.5 * dot_nt(vw[...], normed)
        lat_out[:, rs] = lat
        xlat[0:HDIM, rs] = lat
        return c

    lax.fori_loop(0, toks // BLK, tail_rows, 0)

    outgoing[...] = dot_nt(onehot[...], xlat[...].astype(BF)).astype(BF)

    def out_copy(k):
        to = lax.rem(me + k, n)
        return remote(
            outgoing.at[pl.ds(pl.multiple_of(to * share, share), share)],
            incoming.at[pl.ds(pl.multiple_of(me * share, share), share)],
            asend.at[k], arecv.at[me], to,
        )

    for k in range(1, n):
        out_copy(k).start()
    own = pl.ds(pl.multiple_of(me * share, share), share)
    incoming[own, :] = outgoing[own, :]
    for k in range(1, n):
        src = lax.rem(me + k, n)
        remote(
            outgoing.at[pl.ds(0, share)],
            incoming.at[pl.ds(pl.multiple_of(src * share, share), share)],
            asend.at[k], arecv.at[src], src,
        ).wait_recv()

    got = incoming[...]
    lane_no = iota((8, 128), 1)
    pick = jnp.where(lane_no == HDIM, 1.0, jnp.where(lane_no == HDIM + 1, float(IW), 0.0)).astype(BF)
    pos = dot_nt(pick, got)[0:1, :].astype(jnp.int32)
    onehot[...] = (iota((toks, toks), 0) == jnp.broadcast_to(pos, (toks, toks))).astype(F32).astype(BF)
    tile = dot(onehot[...], got)
    edge = 2 * IW
    wide[edge : edge + toks, :] = tile
    halo_send[0] = tile[:edge].astype(BF)
    halo_send[1] = tile[toks - edge :].astype(BF)

    def halo(k, to):
        return remote(halo_send.at[k], halo_recv.at[k], halo_ssem.at[k], halo_rsem.at[k], to)

    @pl.when(me > 0)
    def _():
        halo(0, me - 1).start()

    @pl.when(me < n - 1)
    def _():
        halo(1, me + 1).start()

    wide[0:edge, :] = jnp.zeros((edge, 128), F32)
    wide[edge + toks :, :] = jnp.zeros((edge, 128), F32)

    @pl.when(me > 0)
    def _():
        halo(1, partner).wait_recv()
        wide[0:edge, :] = halo_recv[1].astype(F32)

    @pl.when(me < n - 1)
    def _():
        halo(0, partner).wait_recv()
        wide[edge + toks :, :] = halo_recv[0].astype(F32)

    ext = toks + 2 * edge
    x = wide[...]
    column = lax.rem(iota((ext, 128), 0), IW)
    lane = iota((ext, 128), 1)
    left = jnp.where(column == 0, 0.0, pltpu.roll(x, 1, 0))
    right = jnp.where(column == IW - 1, 0.0, pltpu.roll(x, ext - 1, 0))
    three = jnp.where(
        lane < HDIM, left,
        jnp.where(lane < 2 * HDIM, pltpu.roll(x, HDIM, 1),
                  jnp.where(lane < 3 * HDIM, pltpu.roll(right, 2 * HDIM, 1), 0.0)),
    )
    three = three.astype(BF)
    mid = toks + 2 * IW
    k3 = 3 * HDIM
    acc = dot(three[0:mid, :k3], w1[0])
    acc = acc + dot(three[IW : IW + mid, :k3], w1[1])
    acc = acc + dot(three[2 * IW : 2 * IW + mid, :k3], w1[2])
    feat = acc / (1.0 + jnp.exp(-acc))
    row_at = iota((mid, 1), 0) // IW
    outside = ((row_at == 0) & (me == 0)) | ((row_at == mid // IW - 1) & (me == n - 1))
    feat = jnp.where(outside, 0.0, feat).astype(BF).astype(F32)
    column = lax.rem(iota((mid, 1), 0), IW)
    shifted[1] = feat.astype(BF)
    shifted[0] = jnp.where(column == 0, 0.0, pltpu.roll(feat, 1, 0)).astype(BF)
    shifted[2] = jnp.where(column == IW - 1, 0.0, pltpu.roll(feat, mid - 1, 0)).astype(BF)
    w2copy.wait()
    out = None
    for a in range(3):
        for b in range(3):
            part = dot(shifted[b, a * IW : a * IW + toks, :], w2[3 * a + b])
            out = part if out is None else out + part
    dec_out[...] = out.astype(BF)

    for k in range(2):

        @pl.when(me >= k + 1)
        def _(k=k):
            lead_copy(k).wait_send()

    for to in range(1, chips):

        @pl.when(chip < to)
        def _(to=to):
            chip_copy(to).wait_send()

    for k in range(1, n):
        out_copy(k).wait_send()

    @pl.when(me > 0)
    def _():
        halo(0, me - 1).wait_send()

    @pl.when(me < n - 1)
    def _():
        halo(1, me + 1).wait_send()


def body(
    hidden_in, noisy_latents, span_ids, tile_map, qkv_weight, out_weight,
    norm_gain, velocity_weight, conv_first, conv_second,
):
    toks, d = hidden_in.shape
    inner = out_weight.shape[0]
    n = lax.axis_size("span")
    pad = -(-(inner + 128) // BLK) * BLK
    ch = conv_first.shape[3]
    wide_cols = -(-qkv_weight.shape[1] // 128) * 128
    pack_cols = max(wide_cols, 2 * inner // 128 * 128 + pad + 128)
    chips = n // 2
    edge = 2 * IW
    mid = toks + 2 * IW
    blocks = -(-qkv_weight.shape[1] // BLK)
    vm, dma = pltpu.VMEM, pltpu.SemaphoreType.DMA
    any_, vmem = pl.BlockSpec(memory_space=pl.ANY), pl.BlockSpec(memory_space=pltpu.VMEM)
    scratch = [
        vm((d, toks), BF), vm((toks, d), BF), vm(qkv_weight.shape, BF), vm(out_weight.shape, BF),
        vm((9, ch, ch), BF), vm((toks, pack_cols), BF),
        vm((toks, pad), BF), vm((toks, pad), BF), vm((toks, pad), BF),
        vm((toks, pad), F32), vm((toks, pad), F32), vm((toks, pad), BF),
        vm((HDIM, pad), F32), vm((HDIM, pad), F32),
        vm((HDIM, pad), BF), vm((HDIM, pad), BF), vm((HDIM, pad), BF), vm((2, HDIM, pad), BF),
        vm((HDIM, pad // 2), BF), vm((chips, HDIM, pad // 2), BF),
        vm((HDIM, pad // 2), BF), vm((HDIM, pad // 2), BF),
        vm((HDIM, pad), F32), vm((HDIM, pad), F32),
        vm((toks, toks), BF), vm((128, toks), F32),
        vm((toks, 128), BF), vm((toks, 128), BF),
        vm((toks + 2 * edge, 128), F32), vm((2, edge, 128), BF), vm((2, edge, 128), BF),
        vm((8, 128), BF), vm((3, mid, ch), BF),
        dma((blocks,)), dma((3,)), dma((2,)), dma((chips,)), dma((chips,)), dma((2,)),
        dma((2,)), dma((2,)), dma((n,)), dma((n,)), dma((2,)), dma((2,)),
    ]
    latents, decoded = pl.pallas_call(
        functools.partial(kernel, (n, toks, d, inner, pad)),
        out_shape=(
            jax.ShapeDtypeStruct(noisy_latents.shape[::-1], F32),
            jax.ShapeDtypeStruct((toks, ch), BF),
        ),
        in_specs=[any_, vmem, vmem, vmem, any_, any_, vmem, vmem, vmem, any_],
        out_specs=(vmem, vmem),
        scratch_shapes=scratch,
        compiler_params=pltpu.CompilerParams(
            collective_id=0, has_side_effects=True, vmem_limit_bytes=60 * 1024 * 1024
        ),
    )(
        hidden_in.T, noisy_latents.T, span_ids.reshape(1, toks), tile_map.reshape(1, -1),
        qkv_weight, out_weight, norm_gain, velocity_weight.T,
        conv_first.reshape(3, 3 * HDIM, ch), conv_second.reshape(9, ch, ch),
    )
    return latents.T, decoded.reshape(toks // IW, IW, ch)


def solution(mesh):
    rows = P(("groups", "span"), None)
    placed = (rows, rows, P(("groups", "span")), P("groups")) + (P(),) * 6
    return jax.shard_map(
        body, mesh=mesh, in_specs=placed,
        out_specs=(rows, P(("groups", "span"), None, None)), check_vma=False,
    )
```
